32 devices in a mesh: groups: 2 (over y), adapter: 16 (over z, x, core).
Axes of the slice: x: 2, y: 2, z: 4, core: 2. Of those that a mesh axis runs over, the one named last changes fastest.
Arguments:
- tokens: bfloat16 [32, 256, 6144], P(('groups', 'adapter')), parts along dimension 0, may hold values from -6 to 6
- base_qkv: bfloat16 [32, 256, 4096], P(('groups', 'adapter')), parts along dimension 0, may hold values from -6 to 6
- cache_keys: bfloat16 [32, 1024, 512], P(('groups', 'adapter')), parts along dimension 0, may hold values from -6 to 6
- cache_values: bfloat16 [32, 1024, 512], P(('groups', 'adapter')), parts along dimension 0, may hold values from -6 to 6
- persona_down: bfloat16 [16, 6144, 64], P('adapter'), may hold values from -0.078125 to 0.078125
- domain_down: bfloat16 [16, 6144, 64], P('adapter'), may hold values from -0.078125 to 0.078125
- persona_up: bfloat16 [16, 4096, 64], P('adapter'), may hold values from -0.29882812 to 0.29882812
- domain_up: bfloat16 [16, 4096, 64], P('adapter'), may hold values from -0.29882812 to 0.29882812
- adapter_ids: int32 [32, 2], P(('groups', 'adapter')), parts along dimension 0, may hold values from 0 to 15
- lengths: int32 [32], P(('groups', 'adapter')), parts along dimension 0, may hold values from 64 to 256, as said below
- offsets: int32 [32], P(('groups', 'adapter')), parts along dimension 0, may hold values from 2 to 1024, as said below
Outputs:
- attended: bfloat16 [32, 256, 3072], P(('groups', 'adapter')), parts along dimension 0
The draws below stay inside these ranges and needn't reach their ends.
There are 2 independent parts, one for each index of `groups`. The reference program is written for one: setup_inputs(seed, part) draws one part's arguments, and reference() takes and returns one part's arrays. A program takes and returns all parts, laid end to end along the dimension named above; an argument that names none is the same for every part. Nothing has to cross between parts.
Inputs may be any that keep to these rules, and one draw needn't show every extreme that they name: `lengths`: each stretch has between 64 and 256 live tokens, the first ones of its slots; some stretch has all 256. `offsets`: each stretch follows between 2 and 1024 cached positions of its prompt, the first ones of its cache; some stretch follows 1024.
All inputs are finite; a program needn't handle non-finite values.
Results may differ from the reference program's by a relative error of at most 0.011.
Values may be sent and summed in bfloat16 or wider, within the bound.
No kernel may reach another device: no remote copies, remote signals or barrier semaphores. Data moves between devices by JAX's collectives and lax.ppermute only.
A program may use at most 128 MiB of HBM per device.

```python
import math
import jax
import jax.numpy as jnp
import numpy as np
from jax import lax

D = 6144
HEAD_DIM = 128
HEADS = 24
KV_HEADS = 4
RANK = 64
STRETCH = 256
CACHE = 1024
QKV = 4096
STRETCHES = 16
ADAPTERS = 16


def drawn_floats(key, shape):
    return jnp.clip(jax.random.normal(key, shape, jnp.float32), -6.0, 6.0)


def draw_base_qkv(key, part):
    values = drawn_floats(jax.random.fold_in(key, 1), (STRETCHES, STRETCH, QKV))
    return values.astype(jnp.bfloat16)


def draw_cache_keys(key, part):
    values = drawn_floats(jax.random.fold_in(key, 2), (STRETCHES, CACHE, KV_HEADS * HEAD_DIM))
    return values.astype(jnp.bfloat16)


def draw_lengths(key, part):
    counts = jax.random.randint(jax.random.fold_in(key, 3), (STRETCHES,), STRETCH // 4, STRETCH + 1, dtype=jnp.int32)
    full_slot = jax.random.randint(jax.random.fold_in(key, 4), (), 0, STRETCHES, dtype=jnp.int32)
    return counts.at[full_slot].set(STRETCH)


def draw_offsets(key, part):
    counts = jax.random.randint(jax.random.fold_in(key, 5), (STRETCHES,), 2, CACHE + 1, dtype=jnp.int32)
    full_slot = jax.random.randint(jax.random.fold_in(key, 6), (), 0, STRETCHES, dtype=jnp.int32)
    return counts.at[full_slot].set(CACHE)


def place_ends(drawn, rng, smallest, high):
    place = [jax.random.randint(jax.random.fold_in(rng, axis), (), 0, length) for axis, length in enumerate(drawn.shape)]
    main_axis = drawn.shape.index(max(drawn.shape))
    next_to = place[:main_axis] + [(place[main_axis] + 1) % drawn.shape[main_axis]] + place[main_axis + 1:]
    return drawn.at[tuple(place)].set(smallest).at[tuple(next_to)].set(high)


def block_scale(rng, dims, pieces, smallest, largest):
    level = 1.0
    for axis_at, shards_of in pieces:
        steps = jax.random.uniform(jax.random.fold_in(jax.random.fold_in(rng, 6), axis_at), (shards_of,), jnp.float32, smallest / len(pieces), largest / len(pieces))
        level = level * jnp.repeat(jnp.exp(steps), dims[axis_at] // shards_of).reshape((-1,) + (1,) * (len(dims) - 1 - axis_at))
    return level


def rank_table(count, skew):
    weights = [(1 << 20) // math.isqrt(rank ** skew) + 1 for rank in range(1, count + 1)]
    scale = 1 + sum(weights) // (1 << 30)
    return np.cumsum(np.array([max(1, weight // scale) for weight in weights]))


def skewed_ids(own_key, extent, number_of, slope):
    grid = rank_table(number_of, slope)
    lot = jax.random.randint(jax.random.fold_in(own_key, 1), extent, 0, int(grid[number_of - 1]))
    rank = jnp.searchsorted(jnp.asarray(grid, jnp.int32), lot, side="right")
    return jax.random.permutation(jax.random.fold_in(own_key, 2), number_of)[rank].astype(jnp.int32)


def scatter_about(key, dims, scale, most, cuts=(), kind=jnp.bfloat16):
    values = jax.random.normal(key, dims, jnp.float32) * scale
    if len(cuts) > 0:
        values = block_scale(key, dims, cuts, -0.22, 0.18) * values
    return jnp.clip(values, min=-most, max=most).astype(kind)


def setup_inputs(seed: int = 0, part: int = 0) -> dict:
    streams_of = jax.random.split(jax.random.key(seed), 12)
    own_keys = jax.random.split(jax.random.fold_in(streams_of[11], part), 12)
    tokens = scatter_about(own_keys[0], (STRETCHES, STRETCH, D), 1.0, 6.0, ((0, 16),))
    base_qkv = draw_base_qkv(jax.random.fold_in(jax.random.fold_in(streams_of[11], part), 71), part)
    cache_keys = draw_cache_keys(jax.random.fold_in(jax.random.fold_in(streams_of[11], part), 71), part)
    cache_values = scatter_about(own_keys[3], (STRETCHES, CACHE, KV_HEADS * HEAD_DIM), 1.0, 6.0, ((0, 16),))
    persona_down = scatter_about(streams_of[4], (ADAPTERS, D, RANK), D ** -0.5, 0.078125, ((0, 16),))
    domain_down = scatter_about(streams_of[5], (ADAPTERS, D, RANK), D ** -0.5, 0.078125, ((0, 16),))
    persona_up = scatter_about(streams_of[6], (ADAPTERS, QKV, RANK), 0.05, 0.29882812, ((0, 16),))
    domain_up = scatter_about(streams_of[7], (ADAPTERS, QKV, RANK), 0.05, 0.29882812, ((0, 16),))
    adapter_ids = place_ends(skewed_ids(own_keys[8], (STRETCHES, 2), ADAPTERS, 2), jax.random.fold_in(own_keys[8], 3), 0, ADAPTERS - 1).astype(jnp.int32)
    lengths = draw_lengths(jax.random.fold_in(jax.random.fold_in(streams_of[11], part), 71), part)
    offsets = draw_offsets(jax.random.fold_in(jax.random.fold_in(streams_of[11], part), 71), part)
    return dict(tokens=tokens, base_qkv=base_qkv, cache_keys=cache_keys, cache_values=cache_values, persona_down=persona_down, domain_down=domain_down, persona_up=persona_up, domain_up=domain_up, adapter_ids=adapter_ids, lengths=lengths, offsets=offsets)


def reference(tokens, base_qkv, cache_keys, cache_values, persona_down, domain_down, persona_up, domain_up, adapter_ids, lengths, offsets):
    query_width = HEADS * HEAD_DIM
    kv_width = KV_HEADS * HEAD_DIM
    group_size = HEADS // KV_HEADS
    key_span = CACHE + STRETCH
    scale = HEAD_DIM ** -0.5

    def one_stretch(operands):
        stretch_tokens, stretch_base, stretch_keys, stretch_values, stretch_ids, stretch_length, stretch_offset = operands
        down_factor = jnp.concatenate([persona_down[stretch_ids[0]], domain_down[stretch_ids[1]]], axis=-1)
        up_factor = jnp.concatenate([persona_up[stretch_ids[0]], domain_up[stretch_ids[1]]], axis=-1)
        low_rank = jnp.dot(stretch_tokens, down_factor, preferred_element_type=jnp.float32).astype(jnp.bfloat16)
        projected = stretch_base.astype(jnp.float32) + jnp.dot(low_rank, up_factor.T, preferred_element_type=jnp.float32)
        queries = lax.optimization_barrier(projected[:, :query_width].astype(jnp.bfloat16))
        fresh_keys = projected[:, query_width:query_width + kv_width].astype(jnp.bfloat16)
        fresh_values = projected[:, query_width + kv_width:].astype(jnp.bfloat16)
        keys_all = lax.optimization_barrier(jnp.concatenate([stretch_keys, fresh_keys], axis=0))
        values_all = lax.optimization_barrier(jnp.concatenate([stretch_values, fresh_values], axis=0))
        grouped = queries.reshape(STRETCH, KV_HEADS, group_size, HEAD_DIM).astype(jnp.float32)
        key_heads = keys_all.reshape(key_span, KV_HEADS, HEAD_DIM).astype(jnp.float32)
        value_heads = values_all.reshape(key_span, KV_HEADS, HEAD_DIM).astype(jnp.float32)
        scores = jnp.einsum("jkgd,lkd->kgjl", grouped, key_heads) * scale
        positions = jnp.arange(key_span, dtype=jnp.int32)
        query_rows = jnp.arange(STRETCH, dtype=jnp.int32)
        visible = jnp.where(positions[None, :] < CACHE, positions[None, :] < stretch_offset, (positions[None, :] - CACHE) <= query_rows[:, None])
        scores = jnp.where(visible[None, None], scores, -jnp.inf)
        row_max = jnp.max(scores, axis=-1, keepdims=True)
        shifted = jnp.exp(scores - row_max)
        row_sum = jnp.sum(shifted, axis=-1)
        weights_bf = lax.optimization_barrier(shifted.astype(jnp.bfloat16))
        mixed = jnp.einsum("kgjl,lkd->jkgd", weights_bf.astype(jnp.float32), value_heads)
        mixed = mixed / jnp.transpose(row_sum, (2, 0, 1))[..., None]
        live = query_rows < stretch_length
        return jnp.where(live[:, None], mixed.reshape(STRETCH, query_width), 0.0).astype(jnp.bfloat16)

    return lax.map(one_stretch, (tokens, base_qkv, cache_keys, cache_values, adapter_ids, lengths, offsets))
```

```python
import functools

import jax
import jax.numpy as jnp
from jax import lax
from jax.experimental import pallas as pl
from jax.experimental.pallas import tpu as pltpu
from jax.sharding import PartitionSpec as P

HEAD_DIM = 128
HEADS = 24
KV_HEADS = 4
GROUP = HEADS // KV_HEADS
STRETCH = 256
CACHE = 1024
ROWS = 8


def attention_kernel(
    offset_ref,
    length_ref,
    low_ref,
    up_q_ref,
    up_k_ref,
    up_v_ref,
    base_q_ref,
    base_k_ref,
    base_v_ref,
    cache_k_ref,
    cache_v_ref,
    out_ref,
    keys,
    values,
    queries,
    bias,
):
    scale = HEAD_DIM ** (-0.5)
    low = low_ref[...]

    @pl.when(pl.program_id(0) == 0)
    def _():
        position = lax.broadcasted_iota(jnp.int32, (STRETCH, CACHE), 1)
        bias[:, :CACHE] = jnp.where(position < offset_ref[0], 0.0, -jnp.inf)
        row = lax.broadcasted_iota(jnp.int32, (STRETCH, STRETCH), 0)
        column = lax.broadcasted_iota(jnp.int32, (STRETCH, STRETCH), 1)
        bias[:, CACHE:] = jnp.where(column <= row, 0.0, -jnp.inf)

    def project(base, up):
        delta = jnp.dot(low, up[...], preferred_element_type=jnp.float32)
        return (base[...].astype(jnp.float32) + delta).astype(jnp.bfloat16)

    keys[:CACHE] = cache_k_ref[...]
    keys[CACHE:] = project(base_k_ref, up_k_ref)
    values[:CACHE] = cache_v_ref[...]
    values[CACHE:] = project(base_v_ref, up_v_ref)
    queries[...] = project(base_q_ref, up_q_ref)
    live = lax.broadcasted_iota(jnp.int32, (STRETCH, HEAD_DIM), 0) < length_ref[0]
    for head in range(GROUP):
        columns = slice(head * HEAD_DIM, (head + 1) * HEAD_DIM)
        scores = lax.dot_general(
            queries[:, columns],
            keys[...],
            (((1,), (1,)), ((), ())),
            preferred_element_type=jnp.float32,
        )
        scores = scores * scale + bias[...]
        row_max = jnp.max(scores, axis=-1, keepdims=True)
        shifted = jnp.exp(scores - row_max)
        row_sum = jnp.sum(shifted, axis=-1, keepdims=True)
        mixed = jnp.dot(
            shifted.astype(jnp.bfloat16), values[...], preferred_element_type=jnp.float32
        )
        mixed = mixed / row_sum
        out_ref[:, columns] = jnp.where(live, mixed, 0.0).astype(out_ref.dtype)


def attention(low, up, base, cache_keys, cache_values, offset, length):
    width = GROUP * HEAD_DIM
    rank2 = low.shape[1]
    key_at = HEADS
    value_at = HEADS + KV_HEADS
    grid_spec = pltpu.PrefetchScalarGridSpec(
        num_scalar_prefetch=2,
        grid=(KV_HEADS,),
        in_specs=[
            pl.BlockSpec((STRETCH, rank2), lambda g, o, n: (0, 0)),
            pl.BlockSpec((rank2, width), lambda g, o, n: (0, g)),
            pl.BlockSpec((rank2, HEAD_DIM), lambda g, o, n: (0, key_at + g)),
            pl.BlockSpec((rank2, HEAD_DIM), lambda g, o, n: (0, value_at + g)),
            pl.BlockSpec((STRETCH, width), lambda g, o, n: (0, g)),
            pl.BlockSpec((STRETCH, HEAD_DIM), lambda g, o, n: (0, key_at + g)),
            pl.BlockSpec((STRETCH, HEAD_DIM), lambda g, o, n: (0, value_at + g)),
            pl.BlockSpec((CACHE, HEAD_DIM), lambda g, o, n: (0, g)),
            pl.BlockSpec((CACHE, HEAD_DIM), lambda g, o, n: (0, g)),
        ],
        out_specs=pl.BlockSpec((STRETCH, width), lambda g, o, n: (0, g)),
        scratch_shapes=[
            pltpu.VMEM((CACHE + STRETCH, HEAD_DIM), jnp.bfloat16),
            pltpu.VMEM((CACHE + STRETCH, HEAD_DIM), jnp.bfloat16),
            pltpu.VMEM((STRETCH, width), jnp.bfloat16),
            pltpu.VMEM((STRETCH, CACHE + STRETCH), jnp.float32),
        ],
    )
    return pl.pallas_call(
        attention_kernel,
        grid_spec=grid_spec,
        out_shape=jax.ShapeDtypeStruct((STRETCH, HEADS * HEAD_DIM), jnp.bfloat16),
        compiler_params=pltpu.CompilerParams(dimension_semantics=("arbitrary",)),
        name="attention",
    )(offset, length, low, up, up, up, base, base, base, cache_keys, cache_values)


def pick_kernel(ids_ref, pool_ref, out_ref, sem):
    copies = [
        pltpu.make_async_copy(pool_ref.at[ids_ref[i]], out_ref.at[i], sem.at[i])
        for i in range(out_ref.shape[0])
    ]
    for copy in copies:
        copy.start()
    for copy in copies:
        copy.wait()


def pick(pool, ids):
    count = ids.shape[0]
    return pl.pallas_call(
        pick_kernel,
        grid_spec=pltpu.PrefetchScalarGridSpec(
            num_scalar_prefetch=1,
            grid=(1,),
            in_specs=[pl.BlockSpec(memory_space=pl.ANY)],
            out_specs=pl.BlockSpec(memory_space=pl.ANY),
            scratch_shapes=[pltpu.SemaphoreType.DMA((count,))],
        ),
        out_shape=jax.ShapeDtypeStruct((count,) + pool.shape[1:], pool.dtype),
        name="pick",
    )(ids, pool)


def fetch_halves(down, up, ids_all):
    group = lax.axis_index("groups")
    index = lax.axis_index("adapter")
    half = index // 8
    rank = down.shape[1]

    def spread(pair):
        mine = jnp.where(group == 0, pair[0], pair[1])
        blocks = mine.reshape(rank // ROWS, ROWS, mine.shape[-1])
        doubled = jnp.concatenate([blocks, blocks], axis=0)
        return lax.all_to_all(doubled, "adapter", 0, 0, tiled=True)

    members = [[g * 16 + h * 8 + k for g in range(2) for k in range(8)] for h in range(2)]
    wanted = lax.dynamic_slice_in_dim(ids_all, half * 8, 8, axis=1)
    wanted = jnp.where(group == 0, wanted[..., 0], wanted[..., 1]).reshape(16)

    def gather(pool):
        picked = pick(pool, wanted)
        got = lax.all_to_all(
            picked, ("groups", "adapter"), 0, 0, tiled=True, axis_index_groups=members
        )
        return got.reshape(2 * rank, pool.shape[-1])

    down_pool = spread(down)
    up_pool = spread(up)
    return gather(down_pool), gather(up_pool)


def fetch_any(down, up, ids_all):
    adapters = ids_all.shape[1]
    group = lax.axis_index("groups")
    rank = down.shape[1]
    parts = adapters // (rank // ROWS)
    wanted = lax.dynamic_index_in_dim(ids_all, group, axis=0, keepdims=False)

    def fetch(pair):
        rows = rank // ROWS
        width = pair.shape[-1] // parts

        def one(factor, ids):
            blocks = factor.reshape(rows, ROWS, parts, width).transpose(0, 2, 1, 3)
            blocks = blocks.reshape(adapters, ROWS, width)
            pool = lax.all_to_all(blocks, "adapter", 0, 0, tiled=True)
            got = lax.all_to_all(jnp.take(pool, ids, axis=0), "adapter", 0, 0, tiled=True)
            got = got.reshape(rows, parts, ROWS, width).transpose(0, 2, 1, 3)
            return got.reshape(rank, parts * width)

        return jnp.concatenate([one(pair[k], wanted[:, k]) for k in range(2)], axis=0)

    return fetch(down), fetch(up)


def body(
    tokens,
    base_qkv,
    cache_keys,
    cache_values,
    persona_down,
    domain_down,
    persona_up,
    domain_up,
    adapter_ids,
    lengths,
    offsets,
    halves,
):
    ids_all = lax.all_gather(adapter_ids, ("groups", "adapter"), axis=0, tiled=True)
    ids_all = ids_all.reshape(2, -1, 2)
    down = (persona_down[0].T, domain_down[0].T)
    up = (persona_up[0].T, domain_up[0].T)
    if halves:
        fetch = fetch_halves
    else:
        fetch = fetch_any
        down = jnp.stack(down)
        up = jnp.stack(up)
    if halves:
        down_mine, up_mine = fetch(_Pair(down), _Pair(up), ids_all)
    else:
        down_mine, up_mine = fetch(down, up, ids_all)
    low = lax.dot_general(
        tokens[0],
        down_mine,
        (((1,), (1,)), ((), ())),
        preferred_element_type=jnp.float32,
    ).astype(jnp.bfloat16)
    out = attention(low, up_mine, base_qkv[0], cache_keys[0], cache_values[0], offsets, lengths)
    return out[None]


class _Pair:
    def __init__(self, items):
        self.items = items
        self.shape = (2,) + items[0].shape

    def __getitem__(self, at):
        return self.items[at]


def solution(mesh):
    both = ("groups", "adapter")
    in_specs = (
        P(both, None, None),
        P(both, None, None),
        P(both, None, None),
        P(both, None, None),
        P("adapter", None, None),
        P("adapter", None, None),
        P("adapter", None, None),
        P("adapter", None, None),
        P(both, None),
        P(both),
        P(both),
    )
    out_specs = P(both, None, None)
    halves = mesh.shape["adapter"] == 16
    return jax.shard_map(
        functools.partial(body, halves=halves),
        mesh=mesh,
        in_specs=in_specs,
        out_specs=out_specs,
        check_vma=False,
    )
```

```python
import functools

import jax
import jax.numpy as jnp
from jax import lax
from jax.experimental import pallas as pl
from jax.experimental.pallas import tpu as pltpu
from jax.sharding import PartitionSpec as P

HEAD_DIM = 128
HEADS = 24
KV_HEADS = 4
GROUP = HEADS // KV_HEADS
STRETCH = 256
CACHE = 1024
ROWS = 8
LANES = 128


def attention_kernel(
    offset_ref,
    length_ref,
    low_ref,
    up_q_ref,
    up_k_ref,
    up_v_ref,
    base_q_ref,
    base_k_ref,
    base_v_ref,
    cache_k_ref,
    cache_v_ref,
    out_ref,
    keys,
    values,
    queries,
    bias,
):
    scale = HEAD_DIM ** (-0.5)
    low = low_ref[...]

    @pl.when(pl.program_id(0) == 0)
    def _():
        position = lax.broadcasted_iota(jnp.int32, (STRETCH, CACHE), 1)
        bias[:, :CACHE] = jnp.where(position < offset_ref[0], 0.0, -jnp.inf)
        row = lax.broadcasted_iota(jnp.int32, (STRETCH, STRETCH), 0)
        column = lax.broadcasted_iota(jnp.int32, (STRETCH, STRETCH), 1)
        bias[:, CACHE:] = jnp.where(column <= row, 0.0, -jnp.inf)

    def project(base, up):
        delta = jnp.dot(low, up[...], preferred_element_type=jnp.float32)
        return (base[...].astype(jnp.float32) + delta).astype(jnp.bfloat16)

    keys[:CACHE] = cache_k_ref[...]
    keys[CACHE:] = project(base_k_ref, up_k_ref)
    values[:CACHE] = cache_v_ref[...]
    values[CACHE:] = project(base_v_ref, up_v_ref)
    queries[...] = project(base_q_ref, up_q_ref)
    live = lax.broadcasted_iota(jnp.int32, (STRETCH, HEAD_DIM), 0) < length_ref[0]
    for head in range(GROUP):
        columns = slice(head * HEAD_DIM, (head + 1) * HEAD_DIM)
        scores = lax.dot_general(
            queries[:, columns],
            keys[...],
            (((1,), (1,)), ((), ())),
            preferred_element_type=jnp.float32,
        )
        scores = scores * scale + bias[...]
        row_max = jnp.max(scores, axis=-1, keepdims=True)
        shifted = jnp.exp(scores - row_max)
        row_sum = jnp.sum(shifted, axis=-1, keepdims=True)
        mixed = jnp.dot(
            shifted.astype(jnp.bfloat16), values[...], preferred_element_type=jnp.float32
        )
        mixed = mixed / row_sum
        out_ref[:, columns] = jnp.where(live, mixed, 0.0).astype(out_ref.dtype)


def attention(low, up, base, cache_keys, cache_values, offset, length):
    width = GROUP * HEAD_DIM
    rank2 = low.shape[1]
    key_at = HEADS
    value_at = HEADS + KV_HEADS
    grid_spec = pltpu.PrefetchScalarGridSpec(
        num_scalar_prefetch=2,
        grid=(KV_HEADS,),
        in_specs=[
            pl.BlockSpec((STRETCH, rank2), lambda g, o, n: (0, 0)),
            pl.BlockSpec((rank2, width), lambda g, o, n: (0, g)),
            pl.BlockSpec((rank2, HEAD_DIM), lambda g, o, n: (0, key_at + g)),
            pl.BlockSpec((rank2, HEAD_DIM), lambda g, o, n: (0, value_at + g)),
            pl.BlockSpec((STRETCH, width), lambda g, o, n: (0, g)),
            pl.BlockSpec((STRETCH, HEAD_DIM), lambda g, o, n: (0, key_at + g)),
            pl.BlockSpec((STRETCH, HEAD_DIM), lambda g, o, n: (0, value_at + g)),
            pl.BlockSpec((CACHE, HEAD_DIM), lambda g, o, n: (0, g)),
            pl.BlockSpec((CACHE, HEAD_DIM), lambda g, o, n: (0, g)),
        ],
        out_specs=pl.BlockSpec((STRETCH, width), lambda g, o, n: (0, g)),
        scratch_shapes=[
            pltpu.VMEM((CACHE + STRETCH, HEAD_DIM), jnp.bfloat16),
            pltpu.VMEM((CACHE + STRETCH, HEAD_DIM), jnp.bfloat16),
            pltpu.VMEM((STRETCH, width), jnp.bfloat16),
            pltpu.VMEM((STRETCH, CACHE + STRETCH), jnp.float32),
        ],
    )
    return pl.pallas_call(
        attention_kernel,
        grid_spec=grid_spec,
        out_shape=jax.ShapeDtypeStruct((STRETCH, HEADS * HEAD_DIM), jnp.bfloat16),
        compiler_params=pltpu.CompilerParams(dimension_semantics=("arbitrary",)),
        name="attention",
    )(offset, length, low, up, up, up, base, base, base, cache_keys, cache_values)


def pick_kernel(ids_ref, pool_ref, out_ref, held, in_sem, out_sem):
    count, _, width = out_ref.shape
    reads = [
        pltpu.make_async_copy(
            pool_ref.at[ids_ref[i], :, pl.ds(0, width)], held.at[i], in_sem.at[i]
        )
        for i in range(count)
    ]
    writes = [
        pltpu.make_async_copy(held.at[i], out_ref.at[i], out_sem.at[i]) for i in range(count)
    ]
    for read in reads:
        read.start()
    for read, write in zip(reads, writes):
        read.wait()
        write.start()
    for write in writes:
        write.wait()


def pick(pool, ids, width):
    count = ids.shape[0]
    rows = pool.shape[1]
    return pl.pallas_call(
        pick_kernel,
        grid_spec=pltpu.PrefetchScalarGridSpec(
            num_scalar_prefetch=1,
            grid=(1,),
            in_specs=[pl.BlockSpec(memory_space=pl.ANY)],
            out_specs=pl.BlockSpec(memory_space=pl.ANY),
            scratch_shapes=[
                pltpu.VMEM((count, rows, width), pool.dtype),
                pltpu.SemaphoreType.DMA((count,)),
                pltpu.SemaphoreType.DMA((count,)),
            ],
        ),
        out_shape=jax.ShapeDtypeStruct((count, rows, width), pool.dtype),
        name="pick",
    )(ids, pool)


def fetch_halves(down, up, ids):
    group = lax.axis_index("groups")
    index = lax.axis_index("adapter")
    rank, down_width = down[0].shape
    up_width = up[0].shape[1]
    blocks = rank // ROWS

    other_ids = lax.ppermute(ids, "groups", [(0, 1), (1, 0)])
    both_ids = jnp.where(group == 0, jnp.stack([ids, other_ids]), jnp.stack([other_ids, ids]))
    note = jnp.pad(
        both_ids.reshape(1, 1, 4).astype(jnp.bfloat16), ((0, 0), (0, ROWS - 1), (0, LANES - 4))
    )
    note = jnp.broadcast_to(note, (blocks, ROWS, LANES))

    def spread(pair, extra=None):
        mine = jnp.where(group == 0, pair[0], pair[1]).reshape(blocks, ROWS, -1)
        if extra is not None:
            mine = jnp.concatenate([mine, extra], axis=-1)
        doubled = jnp.concatenate([mine, mine], axis=0)
        return lax.all_to_all(doubled, "adapter", 0, 0, tiled=True)

    members = [[g * 16 + h * 8 + k for g in range(2) for k in range(8)] for h in range(2)]

    down_pool = spread(down, note)
    up_pool = spread(up)
    notes = down_pool[:, 0, down_width : down_width + 4].astype(jnp.int32)
    lower = index < 8
    notes = jnp.where(lower, notes[:8], notes[8:]).reshape(8, 2, 2)
    wanted = jnp.where(group == 0, notes[..., 0], notes[..., 1]).T.reshape(16)

    def gather(pool, width):
        picked = pick(pool, wanted, width)
        got = lax.all_to_all(
            picked, ("groups", "adapter"), 0, 0, tiled=True, axis_index_groups=members
        )
        return got.reshape(2 * rank, width)

    return gather(down_pool, down_width), gather(up_pool, up_width)


def fetch_any(down, up, ids):
    adapters = lax.axis_size("adapter")
    ids_all = lax.all_gather(ids, ("groups", "adapter"), axis=0, tiled=True)
    ids_all = ids_all.reshape(-1, adapters, 2)
    down = jnp.stack(down)
    up = jnp.stack(up)
    group = lax.axis_index("groups")
    rank = down.shape[1]
    parts = adapters // (rank // ROWS)
    wanted = lax.dynamic_index_in_dim(ids_all, group, axis=0, keepdims=False)

    def fetch(pair):
        rows = rank // ROWS
        width = pair.shape[-1] // parts

        def one(factor, ids):
            blocks = factor.reshape(rows, ROWS, parts, width).transpose(0, 2, 1, 3)
            blocks = blocks.reshape(adapters, ROWS, width)
            pool = lax.all_to_all(blocks, "adapter", 0, 0, tiled=True)
            got = lax.all_to_all(jnp.take(pool, ids, axis=0), "adapter", 0, 0, tiled=True)
            got = got.reshape(rows, parts, ROWS, width).transpose(0, 2, 1, 3)
            return got.reshape(rank, parts * width)

        return jnp.concatenate([one(pair[k], wanted[:, k]) for k in range(2)], axis=0)

    return fetch(down), fetch(up)


def body(
    tokens,
    base_qkv,
    cache_keys,
    cache_values,
    persona_down,
    domain_down,
    persona_up,
    domain_up,
    adapter_ids,
    lengths,
    offsets,
    halves,
):
    down = (persona_down[0].T, domain_down[0].T)
    up = (persona_up[0].T, domain_up[0].T)
    fetch = fetch_halves if halves else fetch_any
    down_mine, up_mine = fetch(down, up, adapter_ids)
    low = lax.dot_general(
        tokens[0],
        down_mine,
        (((1,), (1,)), ((), ())),
        preferred_element_type=jnp.float32,
    ).astype(jnp.bfloat16)
    out = attention(low, up_mine, base_qkv[0], cache_keys[0], cache_values[0], offsets, lengths)
    return out[None]


def solution(mesh):
    both = ("groups", "adapter")
    in_specs = (
        P(both, None, None),
        P(both, None, None),
        P(both, None, None),
        P(both, None, None),
        P("adapter", None, None),
        P("adapter", None, None),
        P("adapter", None, None),
        P("adapter", None, None),
        P(both, None),
        P(both),
        P(both),
    )
    out_specs = P(both, None, None)
    halves = mesh.shape["adapter"] == 16
    return jax.shard_map(
        functools.partial(body, halves=halves),
        mesh=mesh,
        in_specs=in_specs,
        out_specs=out_specs,
        check_vma=False,
    )
```

```python
import functools

import jax
import jax.numpy as jnp
from jax import lax
from jax.experimental import pallas as pl
from jax.experimental.pallas import tpu as pltpu
from jax.sharding import PartitionSpec as P

HEAD_DIM = 128
HEADS = 24
KV_HEADS = 4
GROUP = HEADS // KV_HEADS
STRETCH = 256
CACHE = 1024
ROWS = 8
LANES = 128
CHIPS = 8


def attention_kernel(
    offset_ref,
    length_ref,
    low_ref,
    up_q_ref,
    up_k_ref,
    up_v_ref,
    base_q_ref,
    base_k_ref,
    base_v_ref,
    cache_k_ref,
    cache_v_ref,
    out_ref,
    keys,
    values,
    queries,
    bias,
):
    scale = HEAD_DIM ** (-0.5)
    low = low_ref[...]

    @pl.when(pl.program_id(0) == 0)
    def _():
        position = lax.broadcasted_iota(jnp.int32, (STRETCH, CACHE), 1)
        bias[:, :CACHE] = jnp.where(position < offset_ref[0], 0.0, -jnp.inf)
        row = lax.broadcasted_iota(jnp.int32, (STRETCH, STRETCH), 0)
        column = lax.broadcasted_iota(jnp.int32, (STRETCH, STRETCH), 1)
        bias[:, CACHE:] = jnp.where(column <= row, 0.0, -jnp.inf)

    def project(base, up):
        delta = jnp.dot(low, up[...], preferred_element_type=jnp.float32)
        return (base[...].astype(jnp.float32) + delta).astype(jnp.bfloat16)

    keys[:CACHE] = cache_k_ref[...]
    keys[CACHE:] = project(base_k_ref, up_k_ref)
    values[:CACHE] = cache_v_ref[...]
    values[CACHE:] = project(base_v_ref, up_v_ref)
    queries[...] = project(base_q_ref, up_q_ref)
    live = lax.broadcasted_iota(jnp.int32, (STRETCH, HEAD_DIM), 0) < length_ref[0]
    for head in range(GROUP):
        columns = slice(head * HEAD_DIM, (head + 1) * HEAD_DIM)
        scores = lax.dot_general(
            queries[:, columns],
            keys[...],
            (((1,), (1,)), ((), ())),
            preferred_element_type=jnp.float32,
        )
        scores = scores * scale + bias[...]
        row_max = jnp.max(scores, axis=-1, keepdims=True)
        shifted = jnp.exp(scores - row_max)
        row_sum = jnp.sum(shifted, axis=-1, keepdims=True)
        mixed = jnp.dot(
            shifted.astype(jnp.bfloat16), values[...], preferred_element_type=jnp.float32
        )
        mixed = mixed / row_sum
        out_ref[:, columns] = jnp.where(live, mixed, 0.0).astype(out_ref.dtype)


def attention(low, up, base, cache_keys, cache_values, offset, length):
    width = GROUP * HEAD_DIM
    rank2 = low.shape[1]
    key_at = HEADS
    value_at = HEADS + KV_HEADS
    grid_spec = pltpu.PrefetchScalarGridSpec(
        num_scalar_prefetch=2,
        grid=(KV_HEADS,),
        in_specs=[
            pl.BlockSpec((STRETCH, rank2), lambda g, o, n: (0, 0)),
            pl.BlockSpec((rank2, width), lambda g, o, n: (0, g)),
            pl.BlockSpec((rank2, HEAD_DIM), lambda g, o, n: (0, key_at + g)),
            pl.BlockSpec((rank2, HEAD_DIM), lambda g, o, n: (0, value_at + g)),
            pl.BlockSpec((STRETCH, width), lambda g, o, n: (0, g)),
            pl.BlockSpec((STRETCH, HEAD_DIM), lambda g, o, n: (0, key_at + g)),
            pl.BlockSpec((STRETCH, HEAD_DIM), lambda g, o, n: (0, value_at + g)),
            pl.BlockSpec((CACHE, HEAD_DIM), lambda g, o, n: (0, g)),
            pl.BlockSpec((CACHE, HEAD_DIM), lambda g, o, n: (0, g)),
        ],
        out_specs=pl.BlockSpec((STRETCH, width), lambda g, o, n: (0, g)),
        scratch_shapes=[
            pltpu.VMEM((CACHE + STRETCH, HEAD_DIM), jnp.bfloat16),
            pltpu.VMEM((CACHE + STRETCH, HEAD_DIM), jnp.bfloat16),
            pltpu.VMEM((STRETCH, width), jnp.bfloat16),
            pltpu.VMEM((STRETCH, CACHE + STRETCH), jnp.float32),
        ],
    )
    return pl.pallas_call(
        attention_kernel,
        grid_spec=grid_spec,
        out_shape=jax.ShapeDtypeStruct((STRETCH, HEADS * HEAD_DIM), jnp.bfloat16),
        compiler_params=pltpu.CompilerParams(dimension_semantics=("arbitrary",)),
        name="attention",
    )(offset, length, low, up, up, up, base, base, base, cache_keys, cache_values)


def pick_kernel(ids_ref, pool_ref, out_ref, held, in_sem, out_sem):
    count, _, width = out_ref.shape
    reads = [
        pltpu.make_async_copy(
            pool_ref.at[ids_ref[i], :, pl.ds(0, width)], held.at[i], in_sem.at[i]
        )
        for i in range(count)
    ]
    writes = [
        pltpu.make_async_copy(held.at[i], out_ref.at[i], out_sem.at[i]) for i in range(count)
    ]
    for read in reads:
        read.start()
    for read, write in zip(reads, writes):
        read.wait()
        write.start()
    for write in writes:
        write.wait()


def pick(pool, ids, width):
    count = ids.shape[0]
    rows = pool.shape[1]
    return pl.pallas_call(
        pick_kernel,
        grid_spec=pltpu.PrefetchScalarGridSpec(
            num_scalar_prefetch=1,
            grid=(1,),
            in_specs=[pl.BlockSpec(memory_space=pl.ANY)],
            out_specs=pl.BlockSpec(memory_space=pl.ANY),
            scratch_shapes=[
                pltpu.VMEM((count, rows, width), pool.dtype),
                pltpu.SemaphoreType.DMA((count,)),
                pltpu.SemaphoreType.DMA((count,)),
            ],
        ),
        out_shape=jax.ShapeDtypeStruct((count, rows, width), pool.dtype),
        name="pick",
    )(ids, pool)


def pick_for_chips_kernel(where_ref, ids_ref, own_ref, partner_ref, *refs):
    *out_refs, held, in_sem, out_sem = refs
    width = held.shape[-1]
    chip, core = where_ref[0], where_ref[1]
    reads, writes = [], []
    for m, out_ref in enumerate(out_refs):
        adapter = ids_ref[(m ^ chip) * 2 + core]
        for r, pool_ref in enumerate((own_ref, partner_ref)):
            i = 2 * m + r
            source = pool_ref.at[adapter, :, pl.ds(0, width)]
            reads.append(pltpu.make_async_copy(source, held.at[i], in_sem.at[i]))
            writes.append(pltpu.make_async_copy(held.at[i], out_ref.at[r], out_sem.at[i]))
    for read in reads:
        read.start()
    for read, write in zip(reads, writes):
        read.wait()
        write.start()
    for write in writes:
        write.wait()


def pick_for_chips(where, ids, own, partner, width):
    rows = own.shape[1]
    return pl.pallas_call(
        pick_for_chips_kernel,
        grid_spec=pltpu.PrefetchScalarGridSpec(
            num_scalar_prefetch=2,
            grid=(1,),
            in_specs=[pl.BlockSpec(memory_space=pl.ANY)] * 2,
            out_specs=[pl.BlockSpec(memory_space=pl.ANY)] * CHIPS,
            scratch_shapes=[
                pltpu.VMEM((2 * CHIPS, rows, width), own.dtype),
                pltpu.SemaphoreType.DMA((2 * CHIPS,)),
                pltpu.SemaphoreType.DMA((2 * CHIPS,)),
            ],
        ),
        out_shape=[jax.ShapeDtypeStruct((2, rows, width), own.dtype)] * CHIPS,
        name="pick_for_chips",
    )(where, ids, own, partner)


def place_kernel(where_ref, *refs):
    *piece_refs, out_ref, held, in_sem, out_sem = refs
    chip, core = where_ref[0], where_ref[1]
    reads, writes = [], []
    for m, piece_ref in enumerate(piece_refs):
        for r in range(2):
            i = 2 * m + r
            target = out_ref.at[(m ^ chip) * 2 + (core ^ r)]
            reads.append(pltpu.make_async_copy(piece_ref.at[r], held.at[i], in_sem.at[i]))
            writes.append(pltpu.make_async_copy(held.at[i], target, out_sem.at[i]))
    for read in reads:
        read.start()
    for read, write in zip(reads, writes):
        read.wait()
        write.start()
    for write in writes:
        write.wait()


def place(where, pieces):
    _, rows, width = pieces[0].shape
    dtype = pieces[0].dtype
    return pl.pallas_call(
        place_kernel,
        grid_spec=pltpu.PrefetchScalarGridSpec(
            num_scalar_prefetch=1,
            grid=(1,),
            in_specs=[pl.BlockSpec(memory_space=pl.ANY)] * CHIPS,
            out_specs=pl.BlockSpec(memory_space=pl.ANY),
            scratch_shapes=[
                pltpu.VMEM((2 * CHIPS, rows, width), dtype),
                pltpu.SemaphoreType.DMA((2 * CHIPS,)),
                pltpu.SemaphoreType.DMA((2 * CHIPS,)),
            ],
        ),
        out_shape=jax.ShapeDtypeStruct((2 * CHIPS, rows, width), dtype),
        name="place",
    )(where, *pieces)


def fetch_halves(down, up, ids):
    both = ("groups", "adapter")
    group = lax.axis_index("groups")
    index = lax.axis_index("adapter")
    rank, down_width = down[0].shape
    up_width = up[0].shape[1]
    blocks = rank // ROWS
    slot = index % 8
    where = jnp.stack([group * 4 + slot // 2, slot % 2]).astype(jnp.int32)

    other_ids = lax.ppermute(ids, "groups", [(0, 1), (1, 0)])
    both_ids = jnp.where(group == 0, jnp.stack([ids, other_ids]), jnp.stack([other_ids, ids]))
    note = jnp.pad(
        both_ids.reshape(1, 1, 4).astype(jnp.bfloat16), ((0, 0), (0, ROWS - 1), (0, LANES - 4))
    )
    note = jnp.broadcast_to(note, (blocks, ROWS, LANES))

    def spread(pair, extra=None):
        mine = jnp.where(group == 0, pair[0], pair[1]).reshape(blocks, ROWS, -1)
        if extra is not None:
            mine = jnp.concatenate([mine, extra], axis=-1)
        doubled = jnp.concatenate([mine, mine], axis=0)
        return lax.all_to_all(doubled, "adapter", 0, 0, tiled=True)

    down_pool = spread(down, note)
    up_pool = spread(up)

    notes = down_pool[:, 0, down_width : down_width + 4].astype(jnp.int32)
    notes = jnp.where(index < 8, notes[:8], notes[8:]).reshape(8, 2, 2)
    wanted = jnp.where(group == 0, notes[..., 0], notes[..., 1]).T.reshape(16)

    def xor(value, mask):
        return lax.ppermute(value, both, [(i, i ^ mask) for i in range(32)])

    messages = pick_for_chips(where, wanted, down_pool, xor(down_pool, 1), down_width)
    pieces = [messages[0]]
    for m in range(1, CHIPS):
        pieces.append(xor(messages[m], (m // 4) * 16 + (m % 4) * 2))
    down_mine = place(where, pieces).reshape(2 * rank, down_width)

    members = [[g * 16 + h * 8 + k for g in range(2) for k in range(8)] for h in range(2)]
    picked = pick(up_pool, wanted, up_width)
    got = lax.all_to_all(picked, both, 0, 0, tiled=True, axis_index_groups=members)
    return down_mine, got.reshape(2 * rank, up_width)


def fetch_any(down, up, ids):
    adapters = lax.axis_size("adapter")
    ids_all = lax.all_gather(ids, ("groups", "adapter"), axis=0, tiled=True)
    ids_all = ids_all.reshape(-1, adapters, 2)
    down = jnp.stack(down)
    up = jnp.stack(up)
    group = lax.axis_index("groups")
    rank = down.shape[1]
    parts = adapters // (rank // ROWS)
    wanted = lax.dynamic_index_in_dim(ids_all, group, axis=0, keepdims=False)

    def fetch(pair):
        rows = rank // ROWS
        width = pair.shape[-1] // parts

        def one(factor, ids):
            blocks = factor.reshape(rows, ROWS, parts, width).transpose(0, 2, 1, 3)
            blocks = blocks.reshape(adapters, ROWS, width)
            pool = lax.all_to_all(blocks, "adapter", 0, 0, tiled=True)
            got = lax.all_to_all(jnp.take(pool, ids, axis=0), "adapter", 0, 0, tiled=True)
            got = got.reshape(rows, parts, ROWS, width).transpose(0, 2, 1, 3)
            return got.reshape(rank, parts * width)

        return jnp.concatenate([one(pair[k], wanted[:, k]) for k in range(2)], axis=0)

    return fetch(down), fetch(up)


def body(
    tokens,
    base_qkv,
    cache_keys,
    cache_values,
    persona_down,
    domain_down,
    persona_up,
    domain_up,
    adapter_ids,
    lengths,
    offsets,
    halves,
):
    down = (persona_down[0].T, domain_down[0].T)
    up = (persona_up[0].T, domain_up[0].T)
    fetch = fetch_halves if halves else fetch_any
    down_mine, up_mine = fetch(down, up, adapter_ids)
    low = lax.dot_general(
        tokens[0],
        down_mine,
        (((1,), (1,)), ((), ())),
        preferred_element_type=jnp.float32,
    ).astype(jnp.bfloat16)
    out = attention(low, up_mine, base_qkv[0], cache_keys[0], cache_values[0], offsets, lengths)
    return out[None]


def solution(mesh):
    both = ("groups", "adapter")
    in_specs = (
        P(both, None, None),
        P(both, None, None),
        P(both, None, None),
        P(both, None, None),
        P("adapter", None, None),
        P("adapter", None, None),
        P("adapter", None, None),
        P("adapter", None, None),
        P(both, None),
        P(both),
        P(both),
    )
    out_specs = P(both, None, None)
    halves = mesh.shape["adapter"] == 16
    return jax.shard_map(
        functools.partial(body, halves=halves),
        mesh=mesh,
        in_specs=in_specs,
        out_specs=out_specs,
        check_vma=False,
    )
```
